32 devices in a mesh: shard: 8 (over z, y), pair: 4 (over x, core).
Axes of the slice: x: 2, y: 2, z: 4, core: 2. Of those that a mesh axis runs over, the one named last changes fastest.
Arguments:
- embeds: float32 [8192, 768], P(('shard', 'pair')), may hold values from -256 to 256
- cluster: int32 [8192], P(('shard', 'pair')), may hold values from 0 to 127, as said below
- rank: int32 [8192], P(('shard', 'pair')), may hold values from 0 to 8191, each once
Outputs:
- best: float32 [8192], P(('shard', 'pair'))
The draws below stay inside these ranges and needn't reach their ends.
Inputs may be any that keep to these rules, and one draw needn't show every extreme that they name: Among the rows of one device no group cluster // 16 is named more than 64 times and no quarter of a group more than 16 times; one group, the same for every device, is named exactly 64 times by the rows of every device, each of its quarters exactly 16 times. No two rows share a rank.
All inputs are finite; a program needn't handle non-finite values.
Results may differ from the reference program's by a relative error of at most 0.00031.
Values may be sent and summed in bfloat16 or wider, within the bound.
A program may use at most 64 MiB of HBM per device.

```python
import math
import jax
import jax.numpy as jnp
from jax import lax

D = 768
ROWS_DEV = 256
CL_OWN = 16
CLUSTERS = 128
ROWS = 8192
N_PAIR = 4


def layout_groups(key):
    base = jax.random.fold_in(key, 7)
    devices = ROWS // ROWS_DEV
    groups = CLUSTERS // CL_OWN
    capacity = 2 * ROWS_DEV // groups
    quarter_width = CL_OWN // N_PAIR
    heavy = jax.random.randint(jax.random.fold_in(base, 1), (), 0, groups)
    entries = jnp.arange(groups * capacity, dtype=jnp.int32)
    pool = entries // capacity
    quarter_of = entries % capacity * N_PAIR // capacity

    def one_device(index):
        device_key = jax.random.fold_in(base, index + 2)
        shuffled = jax.random.permutation(jax.random.fold_in(device_key, 0), groups * capacity).astype(jnp.int32)
        priority = jnp.where(pool == heavy, -1, shuffled)
        picked = jnp.argsort(priority, stable=True)[:ROWS_DEV]
        mixing = jax.random.permutation(jax.random.fold_in(device_key, 1), ROWS_DEV)
        homes = pool[picked][mixing]
        quarters = quarter_of[picked][mixing]
        member = jax.random.randint(jax.random.fold_in(device_key, 2), (ROWS_DEV,), 0, quarter_width)
        return (homes * CL_OWN + quarters * quarter_width + member).astype(jnp.int32)
    return jax.vmap(one_device)(jnp.arange(devices, dtype=jnp.int32)).reshape(ROWS)


def draw_cluster(key, part):
    return layout_groups(key)


def draw_embeds(key, part):
    cluster_ids = layout_groups(key)
    inner = jax.random.fold_in(key, 11)
    centers = jax.random.normal(jax.random.fold_in(inner, 0), (CLUSTERS, D), jnp.float32)
    weights = jax.random.uniform(jax.random.fold_in(inner, 1), (ROWS, 1), jnp.float32, 0.2, 2.0)
    scales = jnp.exp(jax.random.uniform(jax.random.fold_in(inner, 2), (ROWS, 1), jnp.float32, 0.0, math.log(10.0)))
    noise = jax.random.normal(jax.random.fold_in(inner, 3), (ROWS, D), jnp.float32)
    values = scales * (weights * centers[cluster_ids] + noise)
    return jnp.clip(values, -256.0, 256.0)


def setup_inputs(seed: int = 0) -> dict:
    streams_of = jax.random.split(jax.random.key(seed), 4)
    return {
        "embeds": draw_embeds(jax.random.fold_in(streams_of[3], 71), 0),
        "cluster": draw_cluster(jax.random.fold_in(streams_of[3], 71), 0),
        "rank": jax.random.permutation(streams_of[2], ROWS).astype(jnp.int32),
    }


def reference(embeds, cluster, rank):
    squares = lax.optimization_barrier(jnp.sum(embeds * embeds, axis=1, keepdims=True))
    unit_rows = (embeds * lax.rsqrt(squares + 1e-06)).astype(jnp.bfloat16)
    groups = CLUSTERS // CL_OWN
    window = 2 * ROWS_DEV * N_PAIR
    home_group = (cluster // CL_OWN).astype(jnp.int32)
    row_order = jnp.argsort(home_group, stable=True).astype(jnp.int32)
    sorted_home = home_group[row_order]
    starts = jnp.searchsorted(sorted_home, jnp.arange(groups, dtype=jnp.int32), side='left').astype(jnp.int32)
    pad_units = jnp.concatenate([unit_rows[row_order], jnp.zeros((window, D), jnp.bfloat16)], axis=0)
    pad_clusters = jnp.concatenate([cluster[row_order], jnp.full((window,), -1, jnp.int32)], axis=0)
    pad_ranks = jnp.concatenate([rank[row_order], jnp.zeros((window,), jnp.int32)], axis=0)

    def one_group(first):
        vectors = lax.dynamic_slice_in_dim(pad_units, first, window, 0).astype(jnp.float32)
        clusters = lax.dynamic_slice_in_dim(pad_clusters, first, window, 0)
        ranks = lax.dynamic_slice_in_dim(pad_ranks, first, window, 0)
        scores = jnp.dot(vectors, vectors.T, preferred_element_type=jnp.float32, precision=lax.Precision.HIGHEST)
        masked = (clusters[:, None] == clusters[None, :]) & (ranks[None, :] < ranks[:, None])
        return lax.optimization_barrier(jnp.max(jnp.where(masked, scores, -1.0), axis=1))
    results = lax.map(one_group, starts)
    position = jnp.arange(ROWS, dtype=jnp.int32) - starts[sorted_home]
    sorted_best = results.reshape(-1)[sorted_home * window + position]
    return jnp.zeros((ROWS,), jnp.float32).at[row_order].set(sorted_best)
```

```python
import functools

import jax
import jax.numpy as jnp
from jax import lax
from jax.experimental import pallas as pl
from jax.experimental.pallas import tpu as pltpu
from jax.sharding import PartitionSpec as P

CL_OWN = 16
LANES = 128
MESH = pl.DeviceIdType.MESH


def log2(value):
    return (value - 1).bit_length()


def kernel(
    pairs, sub, bits, step_bits,
    embeds_in, cluster_in, rank_in, out_ref,
    embeds_ref, cluster_ref, rank_ref,
    send_u, recv_u, send_k, recv_k, answers, returned,
    u_send, u_recv, k_send, k_recv, a_send, a_recv, in_sems, complete,
):
    devices = recv_u.shape[0]
    rows, width = embeds_ref.shape
    per = LANES // sub
    chunks = devices // per
    my_shard, my_pair = lax.axis_index("shard"), lax.axis_index("pair")
    me = my_shard * pairs + my_pair

    def flips(value, count):
        return [(1 << b) * (1 - 2 * ((value // (1 << b)) % 2)) for b in range(count)]

    pair_flips = flips(my_pair, log2(pairs))
    shard_flips = flips(my_shard, log2(devices // pairs))

    def flipped(value, by, changes):
        for b, change in enumerate(changes):
            if by >> b & 1:
                value = value + change
        return value

    def coords(k):
        return (flipped(my_shard, k // pairs, shard_flips), flipped(my_pair, k % pairs, pair_flips))

    def remote(source, target, send, recv, k):
        return pltpu.make_async_remote_copy(
            src_ref=source, dst_ref=target, send_sem=send, recv_sem=recv,
            device_id=coords(k), device_id_type=MESH)

    def send_units(k):
        remote(send_u.at[k], recv_u.at[k], u_send.at[0], u_recv.at[k // per], k).start()

    def send_keys(k):
        remote(send_k.at[k // per], recv_k.at[k], k_send.at[0], k_recv.at[0], k).start()

    def send_answers(k):
        remote(answers.at[k // per], returned.at[k], a_send.at[0], a_recv.at[0], k).start()

    def all_of(buffer, first, stop, send, recv):
        part = buffer.at[pl.ds(first, stop - first)]
        return remote(part, part, send, recv, 1)

    line = [k for k in range(1, devices) if k % per < 2]
    beside = list(range(2, per, 2))

    def signal(semaphore, k):
        pl.semaphore_signal(semaphore, inc=1, device_id=coords(k), device_id_type=MESH)

    barrier = pltpu.get_barrier_semaphore()
    for k in line + beside:
        signal(barrier, k)

    loads = [
        pltpu.make_async_copy(source, target, in_sems.at[k])
        for k, (source, target) in enumerate(
            [(cluster_in, cluster_ref), (rank_in, rank_ref), (embeds_in, embeds_ref)])
    ]
    for load in loads:
        load.start()
    loads[0].wait()
    loads[1].wait()
    cluster = cluster_ref[...]
    key = cluster * (1 << bits) + rank_ref[...]
    bucket = lax.shift_right_logical(cluster, step_bits) ^ me

    def columns(row):
        return jnp.transpose(jnp.broadcast_to(row, (LANES, row.shape[1])))

    bucket_column = columns(bucket)
    lower = lax.broadcasted_iota(jnp.int32, (rows, LANES), 0)
    lane = lax.broadcasted_iota(jnp.int32, (rows, LANES), 1)
    places = []
    for part in range(rows // LANES):
        here = bucket[:, part * LANES:(part + 1) * LANES]
        before = (bucket_column == here) & (lower < lane + part * LANES)
        places.append(jnp.sum(before.astype(jnp.int32), axis=0, keepdims=True))
    slot = bucket * sub + jnp.concatenate(places, axis=1)
    slot_column = columns(slot)
    key_column = columns(key)
    for part in range(chunks):
        found = jnp.where(slot_column == lane + part * LANES, key_column, -1)
        send_k[part] = jnp.max(found, axis=0, keepdims=True)

    loads[2].wait()
    embeds = embeds_ref[...]
    squares = jnp.sum(embeds * embeds, axis=1, keepdims=True)
    unit = (embeds * lax.rsqrt(squares + 1e-06)).astype(jnp.bfloat16)
    chunk_row = lax.broadcasted_iota(jnp.int32, (LANES, rows), 0)

    def place(chunk):
        pick = (slot == chunk_row + chunk * LANES).astype(jnp.float32).astype(jnp.bfloat16)
        placed = jnp.dot(pick, unit, preferred_element_type=jnp.float32).astype(jnp.bfloat16)
        send_u[pl.ds(chunk * per, per)] = placed.reshape(per, sub, width)

    half = chunks // 2
    for chunk in range(half, chunks):
        place(chunk)
    pl.semaphore_wait(barrier, len(line) + len(beside))
    for k in beside:
        signal(complete, k)
    first = [k for k in line if k >= half * per]
    for k in first:
        send_units(k)
    for chunk in range(half):
        place(chunk)
    if beside:
        pl.semaphore_wait(complete, len(beside))
    for k in range(1, devices):
        send_keys(k)
    for k in range(1, devices):
        if k not in first:
            send_units(k)

    recv_u[0] = send_u[0]
    recv_k[0] = send_k[0]

    place_lane = lax.broadcasted_iota(jnp.int32, (per, LANES), 1)
    place_row = lax.broadcasted_iota(jnp.int32, (per, LANES), 0)
    in_place = (place_lane >= place_row * sub) & (place_lane < place_row * sub + sub)

    all_of(recv_k, 1, devices, k_send.at[0], k_recv.at[0]).wait_recv()
    keys, key_columns = [], []
    for chunk in range(chunks):
        part = recv_k[chunk * per:(chunk + 1) * per].reshape(per, LANES)
        keys.append(jnp.max(jnp.where(in_place, part, -1), axis=0, keepdims=True))
        key_columns.append(columns(keys[chunk]))

    def units_of(first, stop):
        return recv_u[first * per:stop * per].reshape((stop - first) * LANES, width)

    def best_of(panel, queries):
        scores = lax.dot_general(
            units_of(*panel), units_of(*queries), (((1,), (1,)), ((), ())), preferred_element_type=jnp.float32)
        panel_keys = jnp.concatenate(key_columns[panel[0]:panel[1]], axis=0)
        found = []
        for index, chunk in enumerate(range(*queries)):
            first = keys[chunk] & (-(1 << bits))
            mask = (panel_keys < keys[chunk]) & (panel_keys >= first)
            part = scores[:, index * LANES:(index + 1) * LANES]
            found.append(jnp.max(jnp.where(mask, part, -1.0), axis=0, keepdims=True))
        return found

    best = []
    for chunk in range(chunks):
        all_of(recv_u, max(chunk * per, 1), (chunk + 1) * per, u_send.at[0], u_recv.at[chunk]).wait_recv()
        new = best_of((0, chunk + 1), (chunk, chunk + 1))
        if chunk == chunks - 1:
            answers[chunk] = new[0]
            for k in range(chunk * per, devices):
                send_answers(k)
        if chunk:
            best = [jnp.maximum(a, b) for a, b in zip(best, best_of((chunk, chunk + 1), (0, chunk)))]
        best = best + new
    for chunk in range(chunks - 2, -1, -1):
        answers[chunk] = best[chunk]
        for k in range(max(chunk * per, 1), (chunk + 1) * per):
            send_answers(k)
    returned[0] = answers[0]

    all_of(recv_k, 1, devices, k_send.at[0], k_recv.at[0]).wait_send()
    all_of(recv_u, 1, devices, u_send.at[0], u_recv.at[0]).wait_send()
    all_of(returned, 1, devices, a_send.at[0], a_recv.at[0]).wait_send()
    all_of(returned, 1, devices, a_send.at[0], a_recv.at[0]).wait_recv()
    by_chunk = []
    for chunk in range(chunks):
        part = returned[chunk * per:(chunk + 1) * per].reshape(per, LANES)
        by_chunk.append(jnp.max(jnp.where(in_place, part, -1.0), axis=0, keepdims=True))
    table = jnp.concatenate(by_chunk + by_chunk, axis=0)
    table_row = lax.broadcasted_iota(jnp.int32, (2 * chunks, LANES), 0)
    for part in range(rows // LANES):
        want = jnp.broadcast_to(slot[:, part * LANES:(part + 1) * LANES], (2 * chunks, LANES))
        found = jnp.take_along_axis(table, want & (LANES - 1), axis=1, mode="promise_in_bounds")
        found = jnp.where(table_row == lax.shift_right_logical(want, log2(LANES)), found, -1.0)
        out_ref[:, part * LANES:(part + 1) * LANES] = jnp.max(found, axis=0, keepdims=True)


def kernel_body(shards, pairs, embeds, cluster, rank):
    rows, width = embeds.shape
    devices = shards * pairs
    sub = 2 * rows // devices
    bits = log2(devices * rows)
    per = LANES // sub
    chunks = devices // per
    vmem = pl.BlockSpec(memory_space=pltpu.VMEM)
    best = pl.pallas_call(
        functools.partial(kernel, pairs, sub, bits, log2(CL_OWN // pairs)),
        out_shape=pltpu.VMEM((1, rows), jnp.float32),
        in_specs=[pl.BlockSpec(memory_space=pl.ANY)] * 3,
        out_specs=vmem,
        scratch_shapes=[
            pltpu.VMEM((rows, width), jnp.float32),
            pltpu.VMEM((1, rows), jnp.int32),
            pltpu.VMEM((1, rows), jnp.int32),
            pltpu.VMEM((devices, sub, width), jnp.bfloat16),
            pltpu.VMEM((devices, sub, width), jnp.bfloat16),
            pltpu.VMEM((chunks, 1, LANES), jnp.int32),
            pltpu.VMEM((devices, 1, LANES), jnp.int32),
            pltpu.VMEM((chunks, 1, LANES), jnp.float32),
            pltpu.VMEM((devices, 1, LANES), jnp.float32),
            pltpu.SemaphoreType.DMA((1,)),
            pltpu.SemaphoreType.DMA((chunks,)),
            pltpu.SemaphoreType.DMA((1,)),
            pltpu.SemaphoreType.DMA((1,)),
            pltpu.SemaphoreType.DMA((1,)),
            pltpu.SemaphoreType.DMA((1,)),
            pltpu.SemaphoreType.DMA((3,)),
            pltpu.SemaphoreType.REGULAR,
        ],
        compiler_params=pltpu.CompilerParams(collective_id=0, has_side_effects=True),
    )(embeds, cluster.reshape(1, rows), rank.reshape(1, rows))
    return best.reshape(rows)


def plain_body(embeds, cluster, rank):
    rows, width = embeds.shape
    pairs = lax.axis_size("pair")
    devices = lax.axis_size("shard") * pairs
    sub = 2 * rows // devices
    slots = devices * sub
    squares = jnp.sum(embeds * embeds, axis=1, keepdims=True)
    unit_rows = (embeds * lax.rsqrt(squares + 1e-06)).astype(jnp.bfloat16)
    bucket = cluster // CL_OWN * pairs + cluster % CL_OWN * pairs // CL_OWN
    index = jnp.arange(rows, dtype=jnp.int32)
    before = (bucket[:, None] == bucket[None, :]) & (index[None, :] < index[:, None])
    slot = bucket * sub + jnp.sum(before.astype(jnp.int32), axis=1)

    def exchange(array):
        blocks = array.reshape((devices, sub) + array.shape[1:])
        return lax.all_to_all(blocks, ("shard", "pair"), 0, 0, tiled=True).reshape(array.shape)

    units = exchange(jnp.zeros((slots, width), jnp.bfloat16).at[slot].set(unit_rows))
    clusters = exchange(jnp.full((slots,), -1, jnp.int32).at[slot].set(cluster))
    ranks = exchange(jnp.zeros((slots,), jnp.int32).at[slot].set(rank))
    scores = jnp.einsum("qd,kd->qk", units, units, preferred_element_type=jnp.float32)
    mask = (clusters[:, None] == clusters[None, :]) & (ranks[None, :] < ranks[:, None])
    return exchange(jnp.max(jnp.where(mask, scores, -1.0), axis=1))[slot]


def solution(mesh):
    shards, pairs = mesh.shape["shard"], mesh.shape["pair"]
    devices = shards * pairs

    def body(embeds, cluster, rank):
        rows, width = embeds.shape
        sub = 2 * rows // devices
        quarter = CL_OWN // pairs
        fits = (
            CL_OWN % pairs == 0 and quarter & (quarter - 1) == 0
            and sub % 16 == 0 and LANES % sub == 0 and devices == 4 * (LANES // sub)
            and rows % LANES == 0 and width % LANES == 0
            and sub < LANES and shards & (shards - 1) == 0
        )
        if fits:
            return kernel_body(shards, pairs, embeds, cluster, rank)
        return plain_body(embeds, cluster, rank)

    in_specs = (P(("shard", "pair"), None), P(("shard", "pair")), P(("shard", "pair")))
    return jax.shard_map(body, mesh=mesh, in_specs=in_specs, out_specs=P(("shard", "pair")), check_vma=False)
```

```python
import functools

import jax
import jax.numpy as jnp
from jax import lax
from jax.experimental import pallas as pl
from jax.experimental.pallas import tpu as pltpu
from jax.sharding import PartitionSpec as P

CL_OWN = 16
LANES = 128
MESH = pl.DeviceIdType.MESH


def log2(value):
    return (value - 1).bit_length()


def kernel(
    pairs, sub, bits, step_bits,
    embeds_in, cluster_in, rank_in, out_ref,
    embeds_ref, cluster_ref, rank_ref,
    send_u, recv_u, send_k, recv_k, answers, returned,
    u_send, u_recv, k_send, k_recv, a_send, a_recv, in_sems, complete,
):
    devices = recv_u.shape[0]
    rows, width = embeds_ref.shape
    per = LANES // sub
    chunks = devices // per
    my_shard, my_pair = lax.axis_index("shard"), lax.axis_index("pair")
    me = my_shard * pairs + my_pair

    def flips(value, count):
        return [(1 << b) * (1 - 2 * ((value // (1 << b)) % 2)) for b in range(count)]

    pair_flips = flips(my_pair, log2(pairs))
    shard_flips = flips(my_shard, log2(devices // pairs))

    def flipped(value, by, changes):
        for b, change in enumerate(changes):
            if by >> b & 1:
                value = value + change
        return value

    def coords(k):
        return (flipped(my_shard, k // pairs, shard_flips), flipped(my_pair, k % pairs, pair_flips))

    def remote(source, target, send, recv, k):
        return pltpu.make_async_remote_copy(
            src_ref=source, dst_ref=target, send_sem=send, recv_sem=recv,
            device_id=coords(k), device_id_type=MESH)

    def send_units(k):
        remote(send_u.at[k], recv_u.at[k], u_send.at[0], u_recv.at[k // per], k).start()

    def send_keys(k):
        remote(send_k.at[k // per], recv_k.at[k], k_send.at[0], k_recv.at[0], k).start()

    def send_answers(k):
        remote(answers.at[k // per], returned.at[k], a_send.at[0], a_recv.at[0], k).start()

    def all_of(buffer, first, stop, send, recv):
        part = buffer.at[pl.ds(first, stop - first)]
        return remote(part, part, send, recv, 1)

    line = [k for k in range(1, devices) if k % per < 2]
    beside = list(range(2, per, 2))

    def signal(semaphore, k):
        pl.semaphore_signal(semaphore, inc=1, device_id=coords(k), device_id_type=MESH)

    barrier = pltpu.get_barrier_semaphore()
    for k in line + beside:
        signal(barrier, k)

    loads = [
        pltpu.make_async_copy(source, target, in_sems.at[k])
        for k, (source, target) in enumerate(
            [(cluster_in, cluster_ref), (rank_in, rank_ref), (embeds_in, embeds_ref)])
    ]
    for load in loads:
        load.start()
    loads[0].wait()
    loads[1].wait()
    cluster = cluster_ref[...]
    key = cluster * (1 << bits) + rank_ref[...]
    bucket = lax.shift_right_logical(cluster, step_bits) ^ me

    def columns(row):
        return jnp.transpose(jnp.broadcast_to(row, (LANES, row.shape[1])))

    bucket_column = columns(bucket)
    lower = lax.broadcasted_iota(jnp.int32, (rows, LANES), 0)
    lane = lax.broadcasted_iota(jnp.int32, (rows, LANES), 1)
    places = []
    for part in range(rows // LANES):
        here = bucket[:, part * LANES:(part + 1) * LANES]
        before = (bucket_column == here) & (lower < lane + part * LANES)
        places.append(jnp.sum(before.astype(jnp.int32), axis=0, keepdims=True))
    slot = bucket * sub + jnp.concatenate(places, axis=1)
    slot_column = columns(slot)
    key_column = columns(key)
    for part in range(chunks):
        found = jnp.where(slot_column == lane + part * LANES, key_column, -1)
        send_k[part] = jnp.max(found, axis=0, keepdims=True)

    loads[2].wait()
    embeds = embeds_ref[...]
    squares = jnp.sum(embeds * embeds, axis=1, keepdims=True)
    unit = (embeds * lax.rsqrt(squares + 1e-06)).astype(jnp.bfloat16)
    chunk_row = lax.broadcasted_iota(jnp.int32, (LANES, rows), 0)

    def place(chunk):
        pick = (slot == chunk_row + chunk * LANES).astype(jnp.float32).astype(jnp.bfloat16)
        placed = jnp.dot(pick, unit, preferred_element_type=jnp.float32).astype(jnp.bfloat16)
        send_u[pl.ds(chunk * per, per)] = placed.reshape(per, sub, width)

    half = chunks // 2
    for chunk in range(half, chunks):
        place(chunk)
    pl.semaphore_wait(barrier, len(line) + len(beside))
    for k in beside:
        signal(complete, k)
    first = [k for k in line if k >= half * per]
    for k in first:
        send_units(k)
    for chunk in range(half):
        place(chunk)
    if beside:
        pl.semaphore_wait(complete, len(beside))
    for k in range(1, devices):
        send_keys(k)
    for k in range(1, devices):
        if k not in first:
            send_units(k)

    recv_u[0] = send_u[0]
    recv_k[0] = send_k[0]

    place_lane = lax.broadcasted_iota(jnp.int32, (per, LANES), 1)
    place_row = lax.broadcasted_iota(jnp.int32, (per, LANES), 0)
    in_place = (place_lane >= place_row * sub) & (place_lane < place_row * sub + sub)

    all_of(recv_k, 1, devices, k_send.at[0], k_recv.at[0]).wait_recv()
    keys, key_columns = [], []
    for chunk in range(chunks):
        part = recv_k[chunk * per:(chunk + 1) * per].reshape(per, LANES)
        keys.append(jnp.max(jnp.where(in_place, part, -1), axis=0, keepdims=True))
        key_columns.append(columns(keys[chunk]))

    def units_of(first, stop):
        return recv_u[first * per:stop * per].reshape((stop - first) * LANES, width)

    def score(chunk):
        scores = lax.dot_general(
            units_of(chunk, chunk + 1), units_of(0, chunk + 1), (((1,), (1,)), ((), ())),
            preferred_element_type=jnp.float32)
        column = key_columns[chunk]
        column_first = column & (-(1 << bits))
        present, arrived = [], None
        for other in range(chunk, -1, -1):
            part = scores[:, other * LANES:(other + 1) * LANES]
            if other < chunk:
                mask = (column < keys[other]) & (column >= (keys[other] & (-(1 << bits))))
                present.append(jnp.max(jnp.where(mask, part, -1.0), axis=0, keepdims=True))
            mask = (keys[other] < column) & (keys[other] >= column_first)
            part = jnp.where(mask, part, -1.0)
            arrived = part if arrived is None else jnp.maximum(arrived, part)
        return present[::-1], jnp.max(jnp.transpose(arrived), axis=0, keepdims=True)

    best = []
    for chunk in range(chunks):
        all_of(recv_u, max(chunk * per, 1), (chunk + 1) * per, u_send.at[0], u_recv.at[chunk]).wait_recv()
        present, arrived = score(chunk)
        best = [jnp.maximum(a, b) for a, b in zip(best, present)] + [arrived]
    answer_order = list(range(chunks - 2, -1, -1)) + [chunks - 1]
    for chunk in answer_order:
        answers[chunk] = best[chunk]
        for k in range(max(chunk * per, 1), (chunk + 1) * per):
            send_answers(k)
    returned[0] = answers[0]

    all_of(recv_k, 1, devices, k_send.at[0], k_recv.at[0]).wait_send()
    all_of(recv_u, 1, devices, u_send.at[0], u_recv.at[0]).wait_send()
    all_of(returned, 1, devices, a_send.at[0], a_recv.at[0]).wait_send()
    all_of(returned, 1, devices, a_send.at[0], a_recv.at[0]).wait_recv()
    by_chunk = []
    for chunk in range(chunks):
        part = returned[chunk * per:(chunk + 1) * per].reshape(per, LANES)
        by_chunk.append(jnp.max(jnp.where(in_place, part, -1.0), axis=0, keepdims=True))
    table = jnp.concatenate(by_chunk + by_chunk, axis=0)
    table_row = lax.broadcasted_iota(jnp.int32, (2 * chunks, LANES), 0)
    for part in range(rows // LANES):
        want = jnp.broadcast_to(slot[:, part * LANES:(part + 1) * LANES], (2 * chunks, LANES))
        found = jnp.take_along_axis(table, want & (LANES - 1), axis=1, mode="promise_in_bounds")
        found = jnp.where(table_row == lax.shift_right_logical(want, log2(LANES)), found, -1.0)
        out_ref[:, part * LANES:(part + 1) * LANES] = jnp.max(found, axis=0, keepdims=True)


def kernel_body(shards, pairs, embeds, cluster, rank):
    rows, width = embeds.shape
    devices = shards * pairs
    sub = 2 * rows // devices
    bits = log2(devices * rows)
    per = LANES // sub
    chunks = devices // per
    vmem = pl.BlockSpec(memory_space=pltpu.VMEM)
    best = pl.pallas_call(
        functools.partial(kernel, pairs, sub, bits, log2(CL_OWN // pairs)),
        out_shape=pltpu.VMEM((1, rows), jnp.float32),
        in_specs=[pl.BlockSpec(memory_space=pl.ANY)] * 3,
        out_specs=vmem,
        scratch_shapes=[
            pltpu.VMEM((rows, width), jnp.float32),
            pltpu.VMEM((1, rows), jnp.int32),
            pltpu.VMEM((1, rows), jnp.int32),
            pltpu.VMEM((devices, sub, width), jnp.bfloat16),
            pltpu.VMEM((devices, sub, width), jnp.bfloat16),
            pltpu.VMEM((chunks, 1, LANES), jnp.int32),
            pltpu.VMEM((devices, 1, LANES), jnp.int32),
            pltpu.VMEM((chunks, 1, LANES), jnp.float32),
            pltpu.VMEM((devices, 1, LANES), jnp.float32),
            pltpu.SemaphoreType.DMA((1,)),
            pltpu.SemaphoreType.DMA((chunks,)),
            pltpu.SemaphoreType.DMA((1,)),
            pltpu.SemaphoreType.DMA((1,)),
            pltpu.SemaphoreType.DMA((1,)),
            pltpu.SemaphoreType.DMA((1,)),
            pltpu.SemaphoreType.DMA((3,)),
            pltpu.SemaphoreType.REGULAR,
        ],
        compiler_params=pltpu.CompilerParams(collective_id=0, has_side_effects=True),
    )(embeds, cluster.reshape(1, rows), rank.reshape(1, rows))
    return best.reshape(rows)


def plain_body(embeds, cluster, rank):
    rows, width = embeds.shape
    pairs = lax.axis_size("pair")
    devices = lax.axis_size("shard") * pairs
    sub = 2 * rows // devices
    slots = devices * sub
    squares = jnp.sum(embeds * embeds, axis=1, keepdims=True)
    unit_rows = (embeds * lax.rsqrt(squares + 1e-06)).astype(jnp.bfloat16)
    bucket = cluster // CL_OWN * pairs + cluster % CL_OWN * pairs // CL_OWN
    index = jnp.arange(rows, dtype=jnp.int32)
    before = (bucket[:, None] == bucket[None, :]) & (index[None, :] < index[:, None])
    slot = bucket * sub + jnp.sum(before.astype(jnp.int32), axis=1)

    def exchange(array):
        blocks = array.reshape((devices, sub) + array.shape[1:])
        return lax.all_to_all(blocks, ("shard", "pair"), 0, 0, tiled=True).reshape(array.shape)

    units = exchange(jnp.zeros((slots, width), jnp.bfloat16).at[slot].set(unit_rows))
    clusters = exchange(jnp.full((slots,), -1, jnp.int32).at[slot].set(cluster))
    ranks = exchange(jnp.zeros((slots,), jnp.int32).at[slot].set(rank))
    scores = jnp.einsum("qd,kd->qk", units, units, preferred_element_type=jnp.float32)
    mask = (clusters[:, None] == clusters[None, :]) & (ranks[None, :] < ranks[:, None])
    return exchange(jnp.max(jnp.where(mask, scores, -1.0), axis=1))[slot]


def solution(mesh):
    shards, pairs = mesh.shape["shard"], mesh.shape["pair"]
    devices = shards * pairs

    def body(embeds, cluster, rank):
        rows, width = embeds.shape
        sub = 2 * rows // devices
        quarter = CL_OWN // pairs
        fits = (
            CL_OWN % pairs == 0 and quarter & (quarter - 1) == 0
            and sub % 16 == 0 and LANES % sub == 0 and devices == 4 * (LANES // sub)
            and rows % LANES == 0 and width % LANES == 0
            and sub < LANES and shards & (shards - 1) == 0
        )
        if fits:
            return kernel_body(shards, pairs, embeds, cluster, rank)
        return plain_body(embeds, cluster, rank)

    in_specs = (P(("shard", "pair"), None), P(("shard", "pair")), P(("shard", "pair")))
    return jax.shard_map(body, mesh=mesh, in_specs=in_specs, out_specs=P(("shard", "pair")), check_vma=False)
```

```python
import functools

import jax
import jax.numpy as jnp
from jax import lax
from jax.experimental import pallas as pl
from jax.experimental.pallas import tpu as pltpu
from jax.sharding import PartitionSpec as P

CL_OWN = 16
LANES = 128
MESH = pl.DeviceIdType.MESH


def log2(value):
    return (value - 1).bit_length()


def kernel(
    pairs, sub, bits, step_bits,
    embeds_in, cluster_in, rank_in, out_ref,
    embeds_ref, cluster_ref, rank_ref,
    send_u, recv_u, send_k, plane_k, recv_k, answers, returned,
    u_send, u_recv, k_send, k_recv, a_send, a_recv, in_sems, complete,
):
    devices = recv_u.shape[0]
    rows, width = embeds_ref.shape
    per = LANES // sub
    chunks = devices // per
    my_shard, my_pair = lax.axis_index("shard"), lax.axis_index("pair")
    me = my_shard * pairs + my_pair

    def flips(value, count):
        return [(1 << b) * (1 - 2 * ((value // (1 << b)) % 2)) for b in range(count)]

    pair_flips = flips(my_pair, log2(pairs))
    shard_flips = flips(my_shard, log2(devices // pairs))

    def flipped(value, by, changes):
        for b, change in enumerate(changes):
            if by >> b & 1:
                value = value + change
        return value

    def coords(k):
        return (flipped(my_shard, k // pairs, shard_flips), flipped(my_pair, k % pairs, pair_flips))

    def remote(source, target, send, recv, k):
        return pltpu.make_async_remote_copy(
            src_ref=source, dst_ref=target, send_sem=send, recv_sem=recv,
            device_id=coords(k), device_id_type=MESH)

    def send_units(k):
        remote(send_u.at[k], recv_u.at[k], u_send.at[0], u_recv.at[k // per], k).start()

    def send_keys(chunk):
        remote(send_k.at[chunk], plane_k.at[chunk], k_send.at[0], k_recv.at[0], chunk * per).start()

    def pass_keys(k):
        remote(plane_k, recv_k.at[k], k_send.at[1], k_recv.at[1], k).start()

    def send_answers(k):
        remote(answers.at[k // per], returned.at[k], a_send.at[0], a_recv.at[0], k).start()

    def all_of(buffer, first, stop, send, recv):
        part = buffer.at[pl.ds(first, stop - first)]
        return remote(part, part, send, recv, 1)

    line = [k for k in range(1, devices) if k % per < 2]
    beside = list(range(2, per, 2))

    def signal(semaphore, k):
        pl.semaphore_signal(semaphore, inc=1, device_id=coords(k), device_id_type=MESH)

    barrier = pltpu.get_barrier_semaphore()
    for k in line + beside:
        signal(barrier, k)

    loads = [
        pltpu.make_async_copy(source, target, in_sems.at[k])
        for k, (source, target) in enumerate(
            [(cluster_in, cluster_ref), (rank_in, rank_ref), (embeds_in, embeds_ref)])
    ]
    for load in loads:
        load.start()
    loads[0].wait()
    loads[1].wait()
    cluster = cluster_ref[...]
    key = cluster * (1 << bits) + rank_ref[...]
    bucket = lax.shift_right_logical(cluster, step_bits) ^ me

    def columns(row):
        return jnp.transpose(jnp.broadcast_to(row, (LANES, row.shape[1])))

    bucket_column = columns(bucket)
    lower = lax.broadcasted_iota(jnp.int32, (rows, LANES), 0)
    lane = lax.broadcasted_iota(jnp.int32, (rows, LANES), 1)
    places = []
    for part in range(rows // LANES):
        here = bucket[:, part * LANES:(part + 1) * LANES]
        before = (bucket_column == here) & (lower < lane + part * LANES)
        places.append(jnp.sum(before.astype(jnp.int32), axis=0, keepdims=True))
    slot = bucket * sub + jnp.concatenate(places, axis=1)
    slot_column = columns(slot)
    key_column = columns(key)
    for part in range(chunks):
        found = jnp.where(slot_column == lane + part * LANES, key_column, -1)
        send_k[part] = jnp.max(found, axis=0, keepdims=True)

    loads[2].wait()
    embeds = embeds_ref[...]
    squares = jnp.sum(embeds * embeds, axis=1, keepdims=True)
    unit = (embeds * lax.rsqrt(squares + 1e-06)).astype(jnp.bfloat16)
    chunk_row = lax.broadcasted_iota(jnp.int32, (LANES, rows), 0)

    def place(chunk):
        pick = (slot == chunk_row + chunk * LANES).astype(jnp.float32).astype(jnp.bfloat16)
        placed = jnp.dot(pick, unit, preferred_element_type=jnp.float32).astype(jnp.bfloat16)
        send_u[pl.ds(chunk * per, per)] = placed.reshape(per, sub, width)

    half = chunks // 2
    for chunk in range(half, chunks):
        place(chunk)
    pl.semaphore_wait(barrier, len(line) + len(beside))
    for k in beside:
        signal(complete, k)
    first = [k for k in line if k >= half * per]
    for chunk in range(1, chunks):
        send_keys(chunk)
    for k in first:
        send_units(k)
    for chunk in range(half):
        place(chunk)
    if beside:
        pl.semaphore_wait(complete, len(beside))
    for k in range(1, devices):
        if k not in first:
            send_units(k)

    plane_k[0] = send_k[0]
    all_of(plane_k, 1, chunks, k_send.at[0], k_recv.at[0]).wait_recv()
    for k in range(1, per):
        pass_keys(k)
    recv_u[0] = send_u[0]
    recv_k[0] = plane_k[...]

    place_lane = lax.broadcasted_iota(jnp.int32, (per, LANES), 1)
    place_row = lax.broadcasted_iota(jnp.int32, (per, LANES), 0)
    in_place = (place_lane >= place_row * sub) & (place_lane < place_row * sub + sub)

    all_of(recv_k, 1, per, k_send.at[1], k_recv.at[1]).wait_recv()
    keys, key_columns = [], []
    for chunk in range(chunks):
        part = recv_k[:, chunk].reshape(per, LANES)
        keys.append(jnp.max(jnp.where(in_place, part, -1), axis=0, keepdims=True))
        key_columns.append(columns(keys[chunk]))

    def units_of(first, stop):
        return recv_u[first * per:stop * per].reshape((stop - first) * LANES, width)

    def score(chunk):
        scores = lax.dot_general(
            units_of(chunk, chunk + 1), units_of(0, chunk + 1), (((1,), (1,)), ((), ())),
            preferred_element_type=jnp.float32)
        column = key_columns[chunk]
        column_first = column & (-(1 << bits))
        present, arrived = [], None
        for other in range(chunk, -1, -1):
            part = scores[:, other * LANES:(other + 1) * LANES]
            if other < chunk:
                mask = (column < keys[other]) & (column >= (keys[other] & (-(1 << bits))))
                present.append(jnp.max(jnp.where(mask, part, -1.0), axis=0, keepdims=True))
            mask = (keys[other] < column) & (keys[other] >= column_first)
            part = jnp.where(mask, part, -1.0)
            arrived = part if arrived is None else jnp.maximum(arrived, part)
        return present[::-1], jnp.max(jnp.transpose(arrived), axis=0, keepdims=True)

    best = []
    for chunk in range(chunks):
        all_of(recv_u, max(chunk * per, 1), (chunk + 1) * per, u_send.at[0], u_recv.at[chunk]).wait_recv()
        present, arrived = score(chunk)
        best = [jnp.maximum(a, b) for a, b in zip(best, present)] + [arrived]
    answer_order = list(range(chunks - 2, -1, -1)) + [chunks - 1]
    for chunk in answer_order:
        answers[chunk] = best[chunk]
        for k in range(max(chunk * per, 1), (chunk + 1) * per):
            send_answers(k)
    returned[0] = answers[0]

    all_of(plane_k, 1, chunks, k_send.at[0], k_recv.at[0]).wait_send()
    all_of(recv_k, 1, per, k_send.at[1], k_recv.at[1]).wait_send()
    all_of(recv_u, 1, devices, u_send.at[0], u_recv.at[0]).wait_send()
    all_of(returned, 1, devices, a_send.at[0], a_recv.at[0]).wait_send()
    all_of(returned, 1, devices, a_send.at[0], a_recv.at[0]).wait_recv()
    by_chunk = []
    for chunk in range(chunks):
        part = returned[chunk * per:(chunk + 1) * per].reshape(per, LANES)
        by_chunk.append(jnp.max(jnp.where(in_place, part, -1.0), axis=0, keepdims=True))
    table = jnp.concatenate(by_chunk + by_chunk, axis=0)
    table_row = lax.broadcasted_iota(jnp.int32, (2 * chunks, LANES), 0)
    for part in range(rows // LANES):
        want = jnp.broadcast_to(slot[:, part * LANES:(part + 1) * LANES], (2 * chunks, LANES))
        found = jnp.take_along_axis(table, want & (LANES - 1), axis=1, mode="promise_in_bounds")
        found = jnp.where(table_row == lax.shift_right_logical(want, log2(LANES)), found, -1.0)
        out_ref[:, part * LANES:(part + 1) * LANES] = jnp.max(found, axis=0, keepdims=True)


def kernel_body(shards, pairs, embeds, cluster, rank):
    rows, width = embeds.shape
    devices = shards * pairs
    sub = 2 * rows // devices
    bits = log2(devices * rows)
    per = LANES // sub
    chunks = devices // per
    vmem = pl.BlockSpec(memory_space=pltpu.VMEM)
    best = pl.pallas_call(
        functools.partial(kernel, pairs, sub, bits, log2(CL_OWN // pairs)),
        out_shape=pltpu.VMEM((1, rows), jnp.float32),
        in_specs=[pl.BlockSpec(memory_space=pl.ANY)] * 3,
        out_specs=vmem,
        scratch_shapes=[
            pltpu.VMEM((rows, width), jnp.float32),
            pltpu.VMEM((1, rows), jnp.int32),
            pltpu.VMEM((1, rows), jnp.int32),
            pltpu.VMEM((devices, sub, width), jnp.bfloat16),
            pltpu.VMEM((devices, sub, width), jnp.bfloat16),
            pltpu.VMEM((chunks, 1, LANES), jnp.int32),
            pltpu.VMEM((chunks, 1, LANES), jnp.int32),
            pltpu.VMEM((per, chunks, 1, LANES), jnp.int32),
            pltpu.VMEM((chunks, 1, LANES), jnp.float32),
            pltpu.VMEM((devices, 1, LANES), jnp.float32),
            pltpu.SemaphoreType.DMA((1,)),
            pltpu.SemaphoreType.DMA((chunks,)),
            pltpu.SemaphoreType.DMA((2,)),
            pltpu.SemaphoreType.DMA((2,)),
            pltpu.SemaphoreType.DMA((1,)),
            pltpu.SemaphoreType.DMA((1,)),
            pltpu.SemaphoreType.DMA((3,)),
            pltpu.SemaphoreType.REGULAR,
        ],
        compiler_params=pltpu.CompilerParams(collective_id=0, has_side_effects=True),
    )(embeds, cluster.reshape(1, rows), rank.reshape(1, rows))
    return best.reshape(rows)


def plain_body(embeds, cluster, rank):
    rows, width = embeds.shape
    pairs = lax.axis_size("pair")
    devices = lax.axis_size("shard") * pairs
    sub = 2 * rows // devices
    slots = devices * sub
    squares = jnp.sum(embeds * embeds, axis=1, keepdims=True)
    unit_rows = (embeds * lax.rsqrt(squares + 1e-06)).astype(jnp.bfloat16)
    bucket = cluster // CL_OWN * pairs + cluster % CL_OWN * pairs // CL_OWN
    index = jnp.arange(rows, dtype=jnp.int32)
    before = (bucket[:, None] == bucket[None, :]) & (index[None, :] < index[:, None])
    slot = bucket * sub + jnp.sum(before.astype(jnp.int32), axis=1)

    def exchange(array):
        blocks = array.reshape((devices, sub) + array.shape[1:])
        return lax.all_to_all(blocks, ("shard", "pair"), 0, 0, tiled=True).reshape(array.shape)

    units = exchange(jnp.zeros((slots, width), jnp.bfloat16).at[slot].set(unit_rows))
    clusters = exchange(jnp.full((slots,), -1, jnp.int32).at[slot].set(cluster))
    ranks = exchange(jnp.zeros((slots,), jnp.int32).at[slot].set(rank))
    scores = jnp.einsum("qd,kd->qk", units, units, preferred_element_type=jnp.float32)
    mask = (clusters[:, None] == clusters[None, :]) & (ranks[None, :] < ranks[:, None])
    return exchange(jnp.max(jnp.where(mask, scores, -1.0), axis=1))[slot]


def solution(mesh):
    shards, pairs = mesh.shape["shard"], mesh.shape["pair"]
    devices = shards * pairs

    def body(embeds, cluster, rank):
        rows, width = embeds.shape
        sub = 2 * rows // devices
        quarter = CL_OWN // pairs
        fits = (
            CL_OWN % pairs == 0 and quarter & (quarter - 1) == 0
            and sub % 16 == 0 and LANES % sub == 0 and devices == 4 * (LANES // sub)
            and rows % LANES == 0 and width % LANES == 0
            and sub < LANES and shards & (shards - 1) == 0
        )
        if fits:
            return kernel_body(shards, pairs, embeds, cluster, rank)
        return plain_body(embeds, cluster, rank)

    in_specs = (P(("shard", "pair"), None), P(("shard", "pair")), P(("shard", "pair")))
    return jax.shard_map(body, mesh=mesh, in_specs=in_specs, out_specs=P(("shard", "pair")), check_vma=False)
```
